256 devices in a mesh: grp: 4 (over y), row: 64 (over z, x, core).
Axes of the slice: x: 4, y: 4, z: 8, core: 2. Of those that a mesh axis runs over, the one named last changes fastest.
Arguments:
- matrix_blocks: bfloat16 [4096, 64, 448], P(('grp', 'row')), may hold values from -0.25 to 0.25
- matrix_columns: int32 [4096, 7], P(('grp', 'row')), may hold values from 0 to 4095, as said below
- prolong_blocks: bfloat16 [4096, 64, 256], P(('grp', 'row')), may hold values from -1.3984375 to 1.3984375
- prolong_columns: int32 [4096, 4], replicated, may hold values from 0 to 511, as said below
Outputs:
- galerkin: bfloat16 [512, 64, 896], P('row')
The draws below stay inside these ranges and needn't reach their ends.
Inputs may be any that keep to these rules, and one draw needn't show every extreme that they name: `matrix_columns`: slot 0 of row i is i itself; the other slots of a row are distinct fine block rows within [(q - 1) * 16, (q + 2) * 16) modulo 4096, q = i // 16. `prolong_columns`: slot 0 of row j is its own aggregate j // 8; the other slots are distinct coarse blocks within [(q - 1) * 2, (q + 2) * 2) modulo 512, q = j // 16.
All inputs are finite; a program needn't handle non-finite values.
Results may differ from the reference program's by a relative error of at most 0.005.
Values may be sent and summed in bfloat16 or wider, within the bound.
No kernel may reach another device: no remote copies, remote signals or barrier semaphores. Data moves between devices by JAX's collectives and lax.ppermute only.
A program may use at most 64 MiB of HBM per device.

```python
import jax
import jax.numpy as jnp
from jax import lax

BS = 64
KA = 7
KP = 4
AGS = 8
NF_DEV = 16
NA = 2
NFINE = 4096
NCOARSE = 512
N_GRP = 4
N_ROW = 64


def distinct_picks(key, count_rows, candidates, picks, own_slot):
    scores = jax.random.randint(key, (count_rows, candidates), 0, 1 << 20, dtype=jnp.int32)
    slot_ids = jnp.arange(candidates, dtype=jnp.int32)[None, :]
    scores = scores * candidates + slot_ids
    scores = jnp.where(slot_ids == own_slot[:, None], -1, scores)
    return lax.top_k(scores, picks)[1].astype(jnp.int32)


def draw_matrix_columns(key, part):
    row_ids = jnp.arange(NFINE, dtype=jnp.int32)
    group_ids = row_ids // NF_DEV
    own_slot = NF_DEV + row_ids % NF_DEV
    picked = distinct_picks(jax.random.fold_in(key, 11), NFINE, 3 * NF_DEV, KA - 1, own_slot)
    others = jnp.mod((group_ids[:, None] - 1) * NF_DEV + picked, NFINE)
    return jnp.concatenate([row_ids[:, None], others], axis=1).astype(jnp.int32)


def draw_prolong_columns(key, part):
    row_ids = jnp.arange(NFINE, dtype=jnp.int32)
    group_ids = row_ids // NF_DEV
    own_aggregate = row_ids // AGS
    own_slot = NA + own_aggregate % NA
    picked = distinct_picks(jax.random.fold_in(key, 23), NFINE, 3 * NA, KP - 1, own_slot)
    others = jnp.mod((group_ids[:, None] - 1) * NA + picked, NCOARSE)
    return jnp.concatenate([own_aggregate[:, None], others], axis=1).astype(jnp.int32)


def steps_of(stream_key, shape, cuts, smallest, high):
    factor_of, own = 1.0, jax.random.fold_in(stream_key, 6)
    for dim, parts in cuts:
        heights = jnp.exp(jax.random.uniform(jax.random.fold_in(own, dim), (parts,), jnp.float32, smallest / len(cuts), high / len(cuts)))
        factor_of = factor_of * jnp.repeat(heights, shape[dim] // parts).reshape([-1 if axis == dim else 1 for axis in range(len(shape))])
    return factor_of


def gaussian(rng, dims, spread, reach, split=(), held_as=jnp.bfloat16):
    level = steps_of(rng, dims, split, -0.22, 0.18) if split else 1.0
    array = jax.random.normal(rng, dims, jnp.float32) * spread * level
    return jnp.minimum(jnp.maximum(array, -reach), reach).astype(held_as)


def setup_inputs(seed: int = 0) -> dict:
    keys = jax.random.split(jax.random.key(seed), 5)
    matrix_blocks = gaussian(keys[0], (NFINE, BS, KA * BS), (KA * BS) ** -0.5, 0.25, ((0, 256),))
    matrix_columns = draw_matrix_columns(jax.random.fold_in(keys[4], 71), 0)
    prolong_blocks = gaussian(keys[2], (NFINE, BS, KP * BS), 0.22, 1.3984375, ((0, 256),))
    prolong_columns = draw_prolong_columns(jax.random.fold_in(keys[4], 71), 0)
    return dict(matrix_blocks=matrix_blocks, matrix_columns=matrix_columns, prolong_blocks=prolong_blocks, prolong_columns=prolong_columns)


def place_onehot(columns, first_column, span_width, modulus):
    relative = jnp.mod(columns - first_column, modulus).astype(jnp.int32)
    return relative[..., None] == jnp.arange(span_width, dtype=jnp.int32)


def group_products(group, matrix_blocks, matrix_columns, prolong_blocks, prolong_columns):
    halo_first = ((group - 1) * NF_DEV).astype(jnp.int32)
    halo_rows = jnp.mod(halo_first + jnp.arange(3 * NF_DEV, dtype=jnp.int32), NFINE).astype(jnp.int32)
    halo_blocks = jnp.take(prolong_blocks, halo_rows, axis=0)
    halo_columns = jnp.take(prolong_columns, halo_rows, axis=0)
    own_first = (group * NF_DEV).astype(jnp.int32)
    matrix_rows = lax.dynamic_slice_in_dim(matrix_blocks, own_first, NF_DEV, 0)
    own_matrix_columns = lax.dynamic_slice_in_dim(matrix_columns, own_first, NF_DEV, 0)
    local_index = jnp.mod(own_matrix_columns - halo_first, NFINE).astype(jnp.int32)
    gathered = jnp.take(halo_blocks, local_index, axis=0).astype(jnp.float32)
    shaped = matrix_rows.reshape(NF_DEV, BS, KA, BS).astype(jnp.float32)
    block_terms = jnp.einsum("rpkm,rkmn->rpkn", shaped, gathered, precision=lax.Precision.HIGHEST)
    block_terms = block_terms.reshape(NF_DEV, BS, KA, KP, BS)
    selector = place_onehot(jnp.take(halo_columns, local_index, axis=0), (group - 2) * NA, 5 * NA, NCOARSE).astype(jnp.float32)
    summed = jnp.einsum("rpkbq,rkbw->rpwq", block_terms, selector, precision=lax.Precision.HIGHEST)
    return summed.astype(jnp.bfloat16).reshape(NF_DEV * BS, 5 * NA * BS)


def reference(matrix_blocks, matrix_columns, prolong_blocks, prolong_columns):
    devices_all = N_GRP * N_ROW
    window_width = 7 * NA * BS
    piece_width = 5 * NA * BS

    def coarse_group(group):
        accumulated = jnp.zeros((NA * BS, window_width), jnp.float32)
        for offset in (-1, 0, 1):
            source = jnp.mod(group + offset, devices_all).astype(jnp.int32)
            products = group_products(source, matrix_blocks, matrix_columns, prolong_blocks, prolong_columns)
            own_first = (source * NF_DEV).astype(jnp.int32)
            own_blocks = lax.dynamic_slice_in_dim(prolong_blocks, own_first, NF_DEV, 0)
            own_columns = lax.dynamic_slice_in_dim(prolong_columns, own_first, NF_DEV, 0)
            selector = place_onehot(own_columns, group * NA, NA, NCOARSE).astype(jnp.float32)
            dense_rows = jnp.einsum("rpbq,rbw->rpwq", own_blocks.reshape(NF_DEV, BS, KP, BS).astype(jnp.float32), selector, precision=lax.Precision.HIGHEST)
            dense_rows = dense_rows.astype(jnp.bfloat16).reshape(NF_DEV * BS, NA * BS)
            contribution = jnp.dot(dense_rows.T, products, preferred_element_type=jnp.float32)
            left_pad = (offset + 1) * NA * BS
            accumulated = accumulated + jnp.pad(contribution, ((0, 0), (left_pad, window_width - piece_width - left_pad)))
        return accumulated.astype(jnp.bfloat16)

    coarse = lax.map(coarse_group, jnp.arange(devices_all, dtype=jnp.int32))
    coarse = coarse.reshape(N_GRP, N_ROW, NA, BS, window_width)
    coarse = jnp.transpose(coarse, (1, 0, 2, 3, 4))
    return coarse.reshape(NCOARSE, BS, window_width)
```

```python
import jax
import jax.numpy as jnp
from jax import lax
from jax.experimental import pallas as pl
from jax.experimental.pallas import tpu as pltpu
from jax.sharding import PartitionSpec as P

AGS = 8
BS = 64
LANES = 128
VMEM_BYTES = 48 * 1024 * 1024


def shifted(value, axis, by):
    peers = lax.axis_size(axis)
    return lax.ppermute(value, axis, [(i, (i + by) % peers) for i in range(peers)])


def spread(blocks_ref, columns_ref, dense_ref):
    rows, _, width = blocks_ref.shape
    low = lax.broadcasted_iota(jnp.int32, (BS, LANES), 1) < BS
    for row in range(rows):
        for slot in range(width // BS):
            block = blocks_ref[row, :, slot * BS : (slot + 1) * BS]
            both = jnp.concatenate([block, block], axis=1)
            column = columns_ref[slot, row]
            place = dense_ref.at[column // 2, row * BS : (row + 1) * BS, :]
            place[...] = jnp.where(low == (column % 2 == 0), both, place[...])


def left_kernel(a_cols_ref, p_cols_ref, a_ref, p_ref, left_ref, own_ref, dense_a_ref, dense_p_ref):
    dense_a_ref[...] = jnp.zeros_like(dense_a_ref)
    dense_p_ref[...] = jnp.zeros_like(dense_p_ref)
    spread(p_ref, p_cols_ref, dense_p_ref)
    spread(a_ref, a_cols_ref, dense_a_ref)
    tiles = dense_p_ref.shape[0]
    p_dense = jnp.concatenate([dense_p_ref[t] for t in range(tiles)], axis=1)
    p_turned = p_dense.T
    groups = left_ref.shape[0]
    per_group = dense_a_ref.shape[0] // groups
    for group in range(groups):
        a_dense = jnp.concatenate(
            [dense_a_ref[group * per_group + t] for t in range(per_group)], axis=1
        )
        part = jnp.dot(p_turned, a_dense, preferred_element_type=jnp.float32)
        left_ref[group] = part.astype(jnp.bfloat16)
    own_ref[...] = jnp.dot(left_ref[1], p_dense, preferred_element_type=jnp.float32)


def right_kernel(
    before_cols_ref, after_cols_ref, before_ref, after_ref, left_ref, own_ref,
    to_before_ref, stay_ref, to_after_ref, dense_before_ref, dense_after_ref,
):
    dense_before_ref[...] = jnp.zeros_like(dense_before_ref)
    dense_after_ref[...] = jnp.zeros_like(dense_after_ref)
    spread(before_ref, before_cols_ref, dense_before_ref)
    spread(after_ref, after_cols_ref, dense_after_ref)

    def term(group, dense_ref):
        dense = jnp.concatenate([dense_ref[t] for t in range(dense_ref.shape[0])], axis=1)
        return jnp.dot(left_ref[group], dense, preferred_element_type=jnp.float32)

    before = term(0, dense_before_ref)
    after = term(2, dense_after_ref)
    own = own_ref[...]
    step = LANES
    summed = jnp.concatenate(
        [
            before[:, :step],
            before[:, step : 2 * step] + own[:, :step],
            before[:, 2 * step :] + own[:, step : 2 * step] + after[:, :step],
            own[:, 2 * step :] + after[:, step : 2 * step],
            after[:, 2 * step :],
        ],
        axis=1,
    )
    rows = stay_ref.shape[0]
    to_before_ref[...] = summed[:rows].astype(to_before_ref.dtype)
    stay_ref[...] = summed[rows : 2 * rows]
    to_after_ref[...] = summed[2 * rows :].astype(to_after_ref.dtype)


def per_device(matrix_blocks, matrix_columns, prolong_blocks, prolong_columns):
    both = ("grp", "row")
    device_count = lax.axis_size(both)
    device_index = lax.axis_index(both)
    rows = matrix_blocks.shape[0]
    aggregates = rows // AGS
    fine_total = device_count * rows
    coarse_total = device_count * aggregates
    side = aggregates * BS
    before_blocks = shifted(prolong_blocks, both, 1)
    after_blocks = shifted(prolong_blocks, both, -1)

    a_cols = jnp.mod(matrix_columns.T - (device_index - 1) * rows, fine_total)
    columns_turned = prolong_columns.T

    def group_cols(offset):
        group = jnp.mod(device_index + offset, device_count)
        cols = lax.dynamic_slice_in_dim(columns_turned, group * rows, rows, 1)
        return jnp.mod(cols - (group - 1) * aggregates, coarse_total)

    bf16 = jnp.bfloat16
    f32 = jnp.float32
    smem = pl.BlockSpec(memory_space=pltpu.SMEM)
    vmem = pl.BlockSpec(memory_space=pltpu.VMEM)
    params = pltpu.CompilerParams(vmem_limit_bytes=VMEM_BYTES)
    left, own = pl.pallas_call(
        left_kernel,
        out_shape=(
            jax.ShapeDtypeStruct((3, 3 * side, rows * BS), bf16),
            jax.ShapeDtypeStruct((3 * side, 3 * side), f32),
        ),
        in_specs=[smem, smem, vmem, vmem],
        out_specs=(vmem, vmem),
        scratch_shapes=[
            pltpu.VMEM((3 * rows * BS // LANES, rows * BS, LANES), bf16),
            pltpu.VMEM((3 * side // LANES, rows * BS, LANES), bf16),
        ],
        compiler_params=params,
        name="left_kernel",
    )(a_cols, group_cols(0), matrix_blocks, prolong_blocks)

    dense = pltpu.VMEM((3 * side // LANES, rows * BS, LANES), bf16)
    to_before, stay, to_after = pl.pallas_call(
        right_kernel,
        out_shape=(
            jax.ShapeDtypeStruct((side, 5 * side), bf16),
            jax.ShapeDtypeStruct((side, 5 * side), f32),
            jax.ShapeDtypeStruct((side, 5 * side), bf16),
        ),
        in_specs=[smem, smem, vmem, vmem, vmem, vmem],
        out_specs=(vmem, vmem, vmem),
        scratch_shapes=[dense, dense],
        compiler_params=params,
        name="right_kernel",
    )(group_cols(-1), group_cols(1), before_blocks, after_blocks, left, own)

    from_before = shifted(to_after, both, 1)
    from_after = shifted(to_before, both, -1)

    def widen(part, offset):
        return jnp.pad(part.astype(f32), ((0, 0), (offset * side, (2 - offset) * side)))

    total = widen(from_before, 0) + widen(stay, 1) + widen(from_after, 2)
    owned = total.astype(bf16).reshape(aggregates, BS, 7 * side)
    return lax.all_gather(owned, "grp", axis=0, tiled=True)


def solution(mesh):
    placed = (
        P(("grp", "row"), None, None),
        P(("grp", "row"), None),
        P(("grp", "row"), None, None),
        P(),
    )
    return jax.shard_map(
        per_device, mesh=mesh, in_specs=placed, out_specs=P("row", None, None), check_vma=False
    )
```

```python
import jax
import jax.numpy as jnp
from jax import lax
from jax.experimental import pallas as pl
from jax.experimental.pallas import tpu as pltpu
from jax.sharding import PartitionSpec as P

AGS = 8
BS = 64
LANES = 128
VMEM_BYTES = 48 * 1024 * 1024
BOTH = ("grp", "row")


def shifted(value, axis, by):
    peers = lax.axis_size(axis)
    return lax.ppermute(value, axis, [(i, (i + by) % peers) for i in range(peers)])


def wrapped(value, total):
    value = jnp.where(value < 0, value + total, value)
    return jnp.where(value >= total, value - total, value)


def spread(blocks_ref, row, column_of, dense_ref):
    low = lax.broadcasted_iota(jnp.int32, (BS, LANES), 1) < BS
    for slot in range(blocks_ref.shape[2] // BS):
        block = blocks_ref[row, :, slot * BS : (slot + 1) * BS]
        twice = jnp.concatenate([block, block], axis=1)
        column = column_of(slot)
        place = dense_ref.at[column // 2, row * BS : (row + 1) * BS, :]
        place[...] = jnp.where(low == (column % 2 == 0), twice, place[...])


def joined(dense_ref, first, count):
    return jnp.concatenate([dense_ref[first + t] for t in range(count)], axis=1)


def columns_copy(columns_hbm, columns_ref, sem, group, rows):
    first = group * rows // LANES * LANES
    return pltpu.make_async_copy(
        columns_hbm.at[:, pl.ds(pl.multiple_of(first, LANES), LANES)], columns_ref, sem
    )


def left_kernel(
    a_cols_ref, columns_hbm, a_hbm, p_hbm, left_ref, own_ref,
    a_ref, p_ref, p_cols_ref, dense_a_ref, dense_p_ref, a_sem, p_sem, c_sem,
):
    rows = a_ref.shape[0]
    group = lax.axis_index(BOTH)
    groups = lax.axis_size(BOTH)
    fine_total = groups * rows
    aggregates = rows // AGS
    copy_c = columns_copy(columns_hbm, p_cols_ref, c_sem, group, rows)
    copy_p = pltpu.make_async_copy(p_hbm, p_ref, p_sem)
    copy_a = pltpu.make_async_copy(a_hbm, a_ref, a_sem)
    copy_c.start()
    copy_p.start()
    copy_a.start()
    dense_p_ref[...] = jnp.zeros_like(dense_p_ref)
    dense_a_ref[...] = jnp.zeros_like(dense_a_ref)
    copy_c.wait()
    copy_p.wait()
    lane = lax.rem(group * rows, LANES)
    for row in range(rows):
        spread(
            p_ref, row,
            lambda slot: wrapped(
                p_cols_ref[slot, lane + row] - (group - 1) * aggregates, groups * aggregates
            ),
            dense_p_ref,
        )
    tiles = dense_p_ref.shape[0]
    p_dense = joined(dense_p_ref, 0, tiles)
    p_turned = p_dense.T
    copy_a.wait()
    for row in range(rows):
        spread(
            a_ref, row,
            lambda slot: wrapped(a_cols_ref[slot, row] - (group - 1) * rows, fine_total),
            dense_a_ref,
        )
    parts = left_ref.shape[0]
    per_part = dense_a_ref.shape[0] // parts
    for part in range(parts):
        a_dense = joined(dense_a_ref, part * per_part, per_part)
        left_ref[part] = jnp.dot(
            p_turned, a_dense, preferred_element_type=jnp.float32
        ).astype(jnp.bfloat16)
    own_ref[...] = jnp.dot(left_ref[1], p_dense, preferred_element_type=jnp.float32)


def right_kernel(
    columns_hbm, before_ref, after_ref, left_ref, own_ref,
    to_before_ref, stay_ref, to_after_ref,
    before_cols_ref, after_cols_ref, dense_before_ref, dense_after_ref, b_sem, a_sem,
):
    rows = before_ref.shape[0]
    group = lax.axis_index(BOTH)
    groups = lax.axis_size(BOTH)
    aggregates = rows // AGS
    before = wrapped(group - 1, groups)
    after = wrapped(group + 1, groups)
    copy_b = columns_copy(columns_hbm, before_cols_ref, b_sem, before, rows)
    copy_a = columns_copy(columns_hbm, after_cols_ref, a_sem, after, rows)
    copy_b.start()
    copy_a.start()
    dense_before_ref[...] = jnp.zeros_like(dense_before_ref)
    dense_after_ref[...] = jnp.zeros_like(dense_after_ref)
    copy_b.wait()
    copy_a.wait()

    def fill(blocks_ref, cols_ref, source, dense_ref):
        lane = lax.rem(source * rows, LANES)
        for row in range(rows):
            spread(
                blocks_ref, row,
                lambda slot: wrapped(
                    cols_ref[slot, lane + row] - (source - 1) * aggregates, groups * aggregates
                ),
                dense_ref,
            )

    fill(before_ref, before_cols_ref, before, dense_before_ref)
    fill(after_ref, after_cols_ref, after, dense_after_ref)

    def term(part, dense_ref):
        dense = joined(dense_ref, 0, dense_ref.shape[0])
        return jnp.dot(left_ref[part], dense, preferred_element_type=jnp.float32)

    first = term(0, dense_before_ref)
    last = term(2, dense_after_ref)
    own = own_ref[...]
    step = LANES
    summed = jnp.concatenate(
        [
            first[:, :step],
            first[:, step : 2 * step] + own[:, :step],
            first[:, 2 * step :] + own[:, step : 2 * step] + last[:, :step],
            own[:, 2 * step :] + last[:, step : 2 * step],
            last[:, 2 * step :],
        ],
        axis=1,
    )
    side = stay_ref.shape[0]
    to_before_ref[...] = summed[:side].astype(to_before_ref.dtype)
    stay_ref[...] = summed[side : 2 * side]
    to_after_ref[...] = summed[2 * side :].astype(to_after_ref.dtype)


def assembled(pieces, offsets, rows, shape):
    def place_kernel(*refs):
        out_hbm, sems = refs[len(pieces)], refs[len(pieces) + 1]
        own = lax.axis_index("grp")
        size = lax.axis_size("grp")
        per_member = shape[0] // size
        copies = []
        for n in range(len(pieces)):
            first = lax.rem(own + offsets[n] + size, size) * per_member + rows[n]
            place = out_hbm.at[pl.ds(first, pieces[n].shape[0])]
            copies.append(pltpu.make_async_copy(refs[n], place, sems.at[n]))
        for copy in copies:
            copy.start()
        for copy in copies:
            copy.wait()

    vmem = pl.BlockSpec(memory_space=pltpu.VMEM)
    return pl.pallas_call(
        place_kernel,
        out_shape=jax.ShapeDtypeStruct(shape, jnp.bfloat16),
        in_specs=[vmem] * len(pieces),
        out_specs=pl.BlockSpec(memory_space=pltpu.HBM),
        scratch_shapes=[pltpu.SemaphoreType.DMA((len(pieces),))],
        compiler_params=pltpu.CompilerParams(vmem_limit_bytes=VMEM_BYTES),
        name="place_kernel",
    )(*pieces)


def per_device(matrix_blocks, matrix_columns, prolong_blocks, prolong_columns):
    rows = matrix_blocks.shape[0]
    aggregates = rows // AGS
    side = aggregates * BS
    before_blocks = shifted(prolong_blocks, BOTH, 1)
    after_blocks = shifted(prolong_blocks, BOTH, -1)
    columns_turned = pltpu.with_memory_space_constraint(prolong_columns.T, pltpu.HBM)
    matrix_kept = pltpu.with_memory_space_constraint(matrix_blocks, pltpu.HBM)
    prolong_kept = pltpu.with_memory_space_constraint(prolong_blocks, pltpu.HBM)
    matrix_turned = pltpu.with_memory_space_constraint(matrix_columns.T, pltpu.HBM)

    bf16 = jnp.bfloat16
    f32 = jnp.float32
    smem = pl.BlockSpec(memory_space=pltpu.SMEM)
    vmem = pl.BlockSpec(memory_space=pltpu.VMEM)
    hbm = pl.BlockSpec(memory_space=pltpu.HBM)
    sem = pltpu.SemaphoreType.DMA(())
    params = pltpu.CompilerParams(vmem_limit_bytes=VMEM_BYTES)
    columns_scratch = pltpu.SMEM((prolong_columns.shape[1], LANES), jnp.int32)
    dense = pltpu.VMEM((3 * side // LANES, rows * BS, LANES), bf16)
    left, own = pl.pallas_call(
        left_kernel,
        out_shape=(
            jax.ShapeDtypeStruct((3, 3 * side, rows * BS), bf16),
            jax.ShapeDtypeStruct((3 * side, 3 * side), f32),
        ),
        in_specs=[smem, hbm, hbm, hbm],
        out_specs=(vmem, vmem),
        scratch_shapes=[
            pltpu.VMEM(matrix_blocks.shape, bf16),
            pltpu.VMEM(prolong_blocks.shape, bf16),
            columns_scratch,
            pltpu.VMEM((3 * rows * BS // LANES, rows * BS, LANES), bf16),
            dense,
            sem, sem, sem,
        ],
        compiler_params=params,
        name="left_kernel",
    )(matrix_turned, columns_turned, matrix_kept, prolong_kept)

    to_before, stay, to_after = pl.pallas_call(
        right_kernel,
        out_shape=(
            jax.ShapeDtypeStruct((side, 5 * side), bf16),
            jax.ShapeDtypeStruct((side, 5 * side), f32),
            jax.ShapeDtypeStruct((side, 5 * side), bf16),
        ),
        in_specs=[hbm, vmem, vmem, vmem, vmem],
        out_specs=(vmem, vmem, vmem),
        scratch_shapes=[columns_scratch, columns_scratch, dense, dense, sem, sem],
        compiler_params=params,
        name="right_kernel",
    )(columns_turned, before_blocks, after_blocks, left, own)

    from_before = shifted(to_after, BOTH, 1)
    from_after = shifted(to_before, BOTH, -1)

    def widen(part, offset):
        return jnp.pad(part.astype(f32), ((0, 0), (offset * side, (2 - offset) * side)))

    total = widen(from_before, 0) + widen(stay, 1) + widen(from_after, 2)
    owned = total.astype(bf16).reshape(aggregates, BS, 7 * side)
    shape = (lax.axis_size("grp") * aggregates, BS, 7 * side)
    pieces = [owned] + [shifted(owned, "grp", by) for by in (1, -1, 2)]
    return assembled(pieces, (0, -1, 1, 2), (0, 0, 0, 0), shape)


def solution(mesh):
    placed = (
        P(("grp", "row"), None, None),
        P(("grp", "row"), None),
        P(("grp", "row"), None, None),
        P(),
    )
    return jax.shard_map(
        per_device, mesh=mesh, in_specs=placed, out_specs=P("row", None, None), check_vma=False
    )
```

```python
import jax
import jax.numpy as jnp
from jax import lax
from jax.experimental import pallas as pl
from jax.experimental.pallas import tpu as pltpu
from jax.sharding import PartitionSpec as P

AGS = 8
BS = 64
LANES = 128
VMEM_BYTES = 48 * 1024 * 1024
BOTH = ("grp", "row")


def shifted(value, axis, by):
    peers = lax.axis_size(axis)
    return lax.ppermute(value, axis, [(i, (i + by) % peers) for i in range(peers)])


def wrapped(value, total):
    value = jnp.where(value < 0, value + total, value)
    return jnp.where(value >= total, value - total, value)


def spread(blocks_ref, row, column_of, dense_ref):
    low = lax.broadcasted_iota(jnp.int32, (BS, LANES), 1) < BS
    for slot in range(blocks_ref.shape[2] // BS):
        block = blocks_ref[row, :, slot * BS : (slot + 1) * BS]
        twice = jnp.concatenate([block, block], axis=1)
        column = column_of(slot)
        place = dense_ref.at[column // 2, row * BS : (row + 1) * BS, :]
        place[...] = jnp.where(low == (column % 2 == 0), twice, place[...])


def joined(dense_ref, first, count):
    return jnp.concatenate([dense_ref[first + t] for t in range(count)], axis=1)


def columns_copy(columns_hbm, columns_ref, sem, group, rows):
    first = group * rows // LANES * LANES
    return pltpu.make_async_copy(
        columns_hbm.at[:, pl.ds(pl.multiple_of(first, LANES), LANES)], columns_ref, sem
    )


def mark(columns_ref, group, groups, rows, mask_ref, first):
    aggregates = rows // AGS
    slots = columns_ref.shape[0]
    block = lax.broadcasted_iota(jnp.int32, mask_ref.shape[1:], 1) // BS
    lane = lax.rem(group * rows, LANES)
    for row in range(rows):
        for slot in range(slots):
            column = wrapped(
                columns_ref[slot, lane + row] - (group - 1) * aggregates, groups * aggregates
            )
            mask_ref[first + row * slots + slot] = jnp.where(block == column, 1.0, 0.0).astype(
                mask_ref.dtype
            )


def dense_rows(blocks_ref, mask_ref, first):
    rows, _, width = blocks_ref.shape
    slots = width // BS
    packed = mask_ref.shape[1]
    low = lax.broadcasted_iota(jnp.int32, (BS, LANES), 1) < BS
    parts = []
    for row in range(rows):
        twice = []
        for pair in range(slots // 2):
            both = blocks_ref[row, :, pair * LANES : (pair + 1) * LANES]
            swapped = jnp.concatenate([both[:, BS:], both[:, :BS]], axis=1)
            twice.append(jnp.where(low, both, swapped))
            twice.append(jnp.where(low, swapped, both))
        tiles = []
        for tile in range(mask_ref.shape[2] // LANES):
            total = None
            for slot in range(slots):
                mask = mask_ref[
                    first + row * slots + slot, :, tile * LANES : (tile + 1) * LANES
                ]
                term = twice[slot].reshape(BS // packed, packed, LANES) * mask[None]
                total = term if total is None else total + term
            tiles.append(total.reshape(BS, LANES))
        parts.append(jnp.concatenate(tiles, axis=1))
    return jnp.concatenate(parts, axis=0)


def left_kernel(
    a_cols_ref, columns_hbm, a_hbm, p_hbm, left_ref, own_ref, mask_ref,
    a_ref, p_ref, p_cols_ref, before_cols_ref, after_cols_ref, dense_a_ref, dense_p_ref,
    a_sem, p_sem, c_sem, before_sem, after_sem,
):
    rows = a_ref.shape[0]
    group = lax.axis_index(BOTH)
    groups = lax.axis_size(BOTH)
    fine_total = groups * rows
    aggregates = rows // AGS
    copy_c = columns_copy(columns_hbm, p_cols_ref, c_sem, group, rows)
    copy_p = pltpu.make_async_copy(p_hbm, p_ref, p_sem)
    copy_a = pltpu.make_async_copy(a_hbm, a_ref, a_sem)
    before = wrapped(group - 1, groups)
    after = wrapped(group + 1, groups)
    copy_before = columns_copy(columns_hbm, before_cols_ref, before_sem, before, rows)
    copy_after = columns_copy(columns_hbm, after_cols_ref, after_sem, after, rows)
    copy_c.start()
    copy_p.start()
    copy_a.start()
    copy_before.start()
    copy_after.start()
    dense_p_ref[...] = jnp.zeros_like(dense_p_ref)
    dense_a_ref[...] = jnp.zeros_like(dense_a_ref)
    copy_c.wait()
    copy_p.wait()
    lane = lax.rem(group * rows, LANES)
    for row in range(rows):
        spread(
            p_ref, row,
            lambda slot: wrapped(
                p_cols_ref[slot, lane + row] - (group - 1) * aggregates, groups * aggregates
            ),
            dense_p_ref,
        )
    tiles = dense_p_ref.shape[0]
    p_dense = joined(dense_p_ref, 0, tiles)
    p_turned = p_dense.T
    copy_a.wait()
    for row in range(rows):
        spread(
            a_ref, row,
            lambda slot: wrapped(a_cols_ref[slot, row] - (group - 1) * rows, fine_total),
            dense_a_ref,
        )
    parts = left_ref.shape[0]
    per_part = dense_a_ref.shape[0] // parts
    for part in range(parts):
        a_dense = joined(dense_a_ref, part * per_part, per_part)
        left_ref[part] = jnp.dot(
            p_turned, a_dense, preferred_element_type=jnp.float32
        ).astype(jnp.bfloat16)
    own_ref[...] = jnp.dot(left_ref[1], p_dense, preferred_element_type=jnp.float32)
    copy_before.wait()
    copy_after.wait()
    mark(before_cols_ref, before, groups, rows, mask_ref, 0)
    mark(after_cols_ref, after, groups, rows, mask_ref, mask_ref.shape[0] // 2)


def right_kernel(
    before_ref, after_ref, mask_ref, left_ref, own_ref, to_before_ref, stay_ref, to_after_ref
):
    def term(part, blocks_ref, first_mask):
        dense = dense_rows(blocks_ref, mask_ref, first_mask)
        return jnp.dot(left_ref[part], dense, preferred_element_type=jnp.float32)

    first = term(0, before_ref, 0)
    last = term(2, after_ref, mask_ref.shape[0] // 2)
    own = own_ref[...]
    step = LANES
    summed = jnp.concatenate(
        [
            first[:, :step],
            first[:, step : 2 * step] + own[:, :step],
            first[:, 2 * step :] + own[:, step : 2 * step] + last[:, :step],
            own[:, 2 * step :] + last[:, step : 2 * step],
            last[:, 2 * step :],
        ],
        axis=1,
    )
    side = stay_ref.shape[0]
    to_before_ref[...] = summed[:side].astype(to_before_ref.dtype)
    stay_ref[...] = summed[side : 2 * side]
    to_after_ref[...] = summed[2 * side :].astype(to_after_ref.dtype)


def placed(out, pieces, offsets, rows, shape):
    given = () if out is None else (out,)

    def place_kernel(*refs):
        out_hbm, sems = refs[-2], refs[-1]
        own = lax.axis_index("grp")
        size = lax.axis_size("grp")
        per_member = shape[0] // size
        copies = []
        for n in range(len(pieces)):
            first = lax.rem(own + offsets[n] + size, size) * per_member + rows[n]
            place = out_hbm.at[pl.ds(first, pieces[n].shape[0])]
            copies.append(pltpu.make_async_copy(refs[len(given) + n], place, sems.at[n]))
        for copy in copies:
            copy.start()
        for copy in copies:
            copy.wait()

    vmem = pl.BlockSpec(memory_space=pltpu.VMEM)
    hbm = pl.BlockSpec(memory_space=pltpu.HBM)
    return pl.pallas_call(
        place_kernel,
        out_shape=jax.ShapeDtypeStruct(shape, jnp.bfloat16),
        in_specs=[hbm] * len(given) + [vmem] * len(pieces),
        out_specs=hbm,
        scratch_shapes=[pltpu.SemaphoreType.DMA((len(pieces),))],
        input_output_aliases={0: 0} if given else {},
        compiler_params=pltpu.CompilerParams(vmem_limit_bytes=VMEM_BYTES),
        name="place_kernel",
    )(*given, *pieces)


def per_device(matrix_blocks, matrix_columns, prolong_blocks, prolong_columns):
    rows = matrix_blocks.shape[0]
    aggregates = rows // AGS
    side = aggregates * BS
    before_blocks = shifted(prolong_blocks, BOTH, 1)
    after_blocks = shifted(prolong_blocks, BOTH, -1)
    columns_turned = pltpu.with_memory_space_constraint(prolong_columns.T, pltpu.HBM)
    matrix_kept = pltpu.with_memory_space_constraint(matrix_blocks, pltpu.HBM)
    prolong_kept = pltpu.with_memory_space_constraint(prolong_blocks, pltpu.HBM)
    matrix_turned = pltpu.with_memory_space_constraint(matrix_columns.T, pltpu.HBM)

    bf16 = jnp.bfloat16
    f32 = jnp.float32
    smem = pl.BlockSpec(memory_space=pltpu.SMEM)
    vmem = pl.BlockSpec(memory_space=pltpu.VMEM)
    hbm = pl.BlockSpec(memory_space=pltpu.HBM)
    sem = pltpu.SemaphoreType.DMA(())
    params = pltpu.CompilerParams(vmem_limit_bytes=VMEM_BYTES)
    columns_scratch = pltpu.SMEM((prolong_columns.shape[1], LANES), jnp.int32)
    dense = pltpu.VMEM((3 * side // LANES, rows * BS, LANES), bf16)
    slots = prolong_columns.shape[1]
    packed = 16
    left, own, masks = pl.pallas_call(
        left_kernel,
        out_shape=(
            jax.ShapeDtypeStruct((3, 3 * side, rows * BS), bf16),
            jax.ShapeDtypeStruct((3 * side, 3 * side), f32),
            jax.ShapeDtypeStruct((2 * rows * slots, packed, 3 * side), bf16),
        ),
        in_specs=[smem, hbm, hbm, hbm],
        out_specs=(vmem, vmem, vmem),
        scratch_shapes=[
            pltpu.VMEM(matrix_blocks.shape, bf16),
            pltpu.VMEM(prolong_blocks.shape, bf16),
            columns_scratch, columns_scratch, columns_scratch,
            pltpu.VMEM((3 * rows * BS // LANES, rows * BS, LANES), bf16),
            dense,
            sem, sem, sem, sem, sem,
        ],
        compiler_params=params,
        name="left_kernel",
    )(matrix_turned, columns_turned, matrix_kept, prolong_kept)

    to_before, stay, to_after = pl.pallas_call(
        right_kernel,
        out_shape=(
            jax.ShapeDtypeStruct((side, 5 * side), bf16),
            jax.ShapeDtypeStruct((side, 5 * side), f32),
            jax.ShapeDtypeStruct((side, 5 * side), bf16),
        ),
        in_specs=[vmem, vmem, vmem, vmem, vmem],
        out_specs=(vmem, vmem, vmem),
        compiler_params=params,
        name="right_kernel",
    )(before_blocks, after_blocks, masks, left, own)

    from_before = shifted(to_after, BOTH, 1)
    from_after = shifted(to_before, BOTH, -1)

    def widen(part, offset):
        return jnp.pad(part.astype(f32), ((0, 0), (offset * side, (2 - offset) * side)))

    total = widen(from_before, 0) + widen(stay, 1) + widen(from_after, 2)
    owned = total.astype(bf16).reshape(aggregates, BS, 7 * side)
    shape = (lax.axis_size("grp") * aggregates, BS, 7 * side)
    below, above, far = [shifted(owned, "grp", by) for by in (1, -1, 2)]
    out = placed(None, [owned, above, far], (0, 1, 2), (0, 0, 0), shape)
    return placed(out, [below], (-1,), (0,), shape)


def solution(mesh):
    placed = (
        P(("grp", "row"), None, None),
        P(("grp", "row"), None),
        P(("grp", "row"), None, None),
        P(),
    )
    return jax.shard_map(
        per_device, mesh=mesh, in_specs=placed, out_specs=P("row", None, None), check_vma=False
    )
```

```python
import jax
import jax.numpy as jnp
from jax import lax
from jax.experimental import pallas as pl
from jax.experimental.pallas import tpu as pltpu
from jax.sharding import PartitionSpec as P

AGS = 8
BS = 64
LANES = 128
VMEM_BYTES = 48 * 1024 * 1024
BOTH = ("grp", "row")


def shifted(value, axis, by):
    peers = lax.axis_size(axis)
    return lax.ppermute(value, axis, [(i, (i + by) % peers) for i in range(peers)])


def wrapped(value, total):
    value = jnp.where(value < 0, value + total, value)
    return jnp.where(value >= total, value - total, value)


def spread(blocks_ref, row, column_of, dense_ref):
    low = lax.broadcasted_iota(jnp.int32, (BS, LANES), 1) < BS
    for slot in range(blocks_ref.shape[2] // BS):
        block = blocks_ref[row, :, slot * BS : (slot + 1) * BS]
        twice = jnp.concatenate([block, block], axis=1)
        column = column_of(slot)
        place = dense_ref.at[column // 2, row * BS : (row + 1) * BS, :]
        place[...] = jnp.where(low == (column % 2 == 0), twice, place[...])


def joined(dense_ref, first, count):
    return jnp.concatenate([dense_ref[first + t] for t in range(count)], axis=1)


def columns_copy(columns_hbm, columns_ref, sem, group, rows):
    first = group * rows // LANES * LANES
    return pltpu.make_async_copy(
        columns_hbm.at[:, pl.ds(pl.multiple_of(first, LANES), LANES)], columns_ref, sem
    )


def mark(columns_ref, group, groups, rows, mask_ref, first):
    aggregates = rows // AGS
    slots = columns_ref.shape[0]
    block = lax.broadcasted_iota(jnp.int32, mask_ref.shape[1:], 1) // BS
    lane = lax.rem(group * rows, LANES)
    low = lax.rem(lax.broadcasted_iota(jnp.int32, mask_ref.shape[1:], 1), LANES) < BS
    for row in range(rows):
        for slot in range(0, slots, 2):
            even, odd = [
                wrapped(columns_ref[n, lane + row] - (group - 1) * aggregates, groups * aggregates)
                for n in (slot, slot + 1)
            ]
            for n, column in enumerate((jnp.where(low, even, odd), jnp.where(low, odd, even))):
                mask_ref[first + row * slots + slot + n] = jnp.where(
                    block == column, 1.0, 0.0
                ).astype(mask_ref.dtype)


def dense_rows(blocks_ref, mask_ref, first):
    rows, _, width = blocks_ref.shape
    slots = width // BS
    packed = mask_ref.shape[1]
    parts = []
    for row in range(rows):
        twice = []
        for pair in range(slots // 2):
            both = blocks_ref[row, :, pair * LANES : (pair + 1) * LANES]
            swapped = jnp.concatenate([both[:, BS:], both[:, :BS]], axis=1)
            twice += [both, swapped]
        tiles = []
        for tile in range(mask_ref.shape[2] // LANES):
            total = None
            for slot in range(slots):
                mask = mask_ref[
                    first + row * slots + slot, :, tile * LANES : (tile + 1) * LANES
                ]
                term = twice[slot].reshape(BS // packed, packed, LANES) * mask[None]
                total = term if total is None else total + term
            tiles.append(total.reshape(BS, LANES))
        parts.append(jnp.concatenate(tiles, axis=1))
    return jnp.concatenate(parts, axis=0)


def left_kernel(
    a_cols_ref, columns_hbm, a_hbm, p_hbm, left_ref, own_ref, mask_ref,
    a_ref, p_ref, p_cols_ref, before_cols_ref, after_cols_ref, dense_a_ref, dense_p_ref,
    a_sem, p_sem, c_sem, before_sem, after_sem,
):
    rows = a_ref.shape[0]
    group = lax.axis_index(BOTH)
    groups = lax.axis_size(BOTH)
    fine_total = groups * rows
    aggregates = rows // AGS
    copy_c = columns_copy(columns_hbm, p_cols_ref, c_sem, group, rows)
    copy_p = pltpu.make_async_copy(p_hbm, p_ref, p_sem)
    copy_a = pltpu.make_async_copy(a_hbm, a_ref, a_sem)
    before = wrapped(group - 1, groups)
    after = wrapped(group + 1, groups)
    copy_before = columns_copy(columns_hbm, before_cols_ref, before_sem, before, rows)
    copy_after = columns_copy(columns_hbm, after_cols_ref, after_sem, after, rows)
    copy_c.start()
    copy_p.start()
    copy_a.start()
    copy_before.start()
    copy_after.start()
    dense_p_ref[...] = jnp.zeros_like(dense_p_ref)
    dense_a_ref[...] = jnp.zeros_like(dense_a_ref)
    copy_c.wait()
    copy_p.wait()
    lane = lax.rem(group * rows, LANES)
    for row in range(rows):
        spread(
            p_ref, row,
            lambda slot: wrapped(
                p_cols_ref[slot, lane + row] - (group - 1) * aggregates, groups * aggregates
            ),
            dense_p_ref,
        )
    tiles = dense_p_ref.shape[0]
    p_dense = joined(dense_p_ref, 0, tiles)
    p_turned = p_dense.T
    copy_a.wait()
    for row in range(rows):
        spread(
            a_ref, row,
            lambda slot: wrapped(a_cols_ref[slot, row] - (group - 1) * rows, fine_total),
            dense_a_ref,
        )
    parts = left_ref.shape[0]
    per_part = dense_a_ref.shape[0] // parts
    for part in range(parts):
        a_dense = joined(dense_a_ref, part * per_part, per_part)
        left_ref[part] = jnp.dot(
            p_turned, a_dense, preferred_element_type=jnp.float32
        ).astype(jnp.bfloat16)
    own_ref[...] = jnp.dot(left_ref[1], p_dense, preferred_element_type=jnp.float32)
    copy_before.wait()
    copy_after.wait()
    mark(before_cols_ref, before, groups, rows, mask_ref, 0)
    mark(after_cols_ref, after, groups, rows, mask_ref, mask_ref.shape[0] // 2)


def right_kernel(
    before_ref, after_ref, mask_ref, left_ref, own_ref, to_before_ref, stay_ref, to_after_ref
):
    def term(part, blocks_ref, first_mask):
        dense = dense_rows(blocks_ref, mask_ref, first_mask)
        return jnp.dot(left_ref[part], dense, preferred_element_type=jnp.float32)

    first = term(0, before_ref, 0)
    last = term(2, after_ref, mask_ref.shape[0] // 2)
    own = own_ref[...]
    step = LANES
    summed = jnp.concatenate(
        [
            first[:, :step],
            first[:, step : 2 * step] + own[:, :step],
            first[:, 2 * step :] + own[:, step : 2 * step] + last[:, :step],
            own[:, 2 * step :] + last[:, step : 2 * step],
            last[:, 2 * step :],
        ],
        axis=1,
    )
    side = stay_ref.shape[0]
    to_before_ref[...] = summed[:side].astype(to_before_ref.dtype)
    stay_ref[...] = summed[side : 2 * side]
    to_after_ref[...] = summed[2 * side :].astype(to_after_ref.dtype)


def placed(out, pieces, offsets, rows, shape):
    given = () if out is None else (out,)

    def place_kernel(*refs):
        out_hbm, sems = refs[-2], refs[-1]
        own = lax.axis_index("grp")
        size = lax.axis_size("grp")
        per_member = shape[0] // size
        copies = []
        for n in range(len(pieces)):
            first = lax.rem(own + offsets[n] + size, size) * per_member + rows[n]
            place = out_hbm.at[pl.ds(first, pieces[n].shape[0])]
            copies.append(pltpu.make_async_copy(refs[len(given) + n], place, sems.at[n]))
        for copy in copies:
            copy.start()
        for copy in copies:
            copy.wait()

    vmem = pl.BlockSpec(memory_space=pltpu.VMEM)
    hbm = pl.BlockSpec(memory_space=pltpu.HBM)
    return pl.pallas_call(
        place_kernel,
        out_shape=jax.ShapeDtypeStruct(shape, jnp.bfloat16),
        in_specs=[hbm] * len(given) + [vmem] * len(pieces),
        out_specs=hbm,
        scratch_shapes=[pltpu.SemaphoreType.DMA((len(pieces),))],
        input_output_aliases={0: 0} if given else {},
        compiler_params=pltpu.CompilerParams(vmem_limit_bytes=VMEM_BYTES),
        name="place_kernel",
    )(*given, *pieces)


def per_device(matrix_blocks, matrix_columns, prolong_blocks, prolong_columns):
    rows = matrix_blocks.shape[0]
    aggregates = rows // AGS
    side = aggregates * BS
    before_blocks = shifted(prolong_blocks, BOTH, 1)
    after_blocks = shifted(prolong_blocks, BOTH, -1)
    columns_turned = pltpu.with_memory_space_constraint(prolong_columns.T, pltpu.HBM)
    matrix_kept = pltpu.with_memory_space_constraint(matrix_blocks, pltpu.HBM)
    prolong_kept = pltpu.with_memory_space_constraint(prolong_blocks, pltpu.HBM)
    matrix_turned = pltpu.with_memory_space_constraint(matrix_columns.T, pltpu.HBM)

    bf16 = jnp.bfloat16
    f32 = jnp.float32
    smem = pl.BlockSpec(memory_space=pltpu.SMEM)
    vmem = pl.BlockSpec(memory_space=pltpu.VMEM)
    hbm = pl.BlockSpec(memory_space=pltpu.HBM)
    sem = pltpu.SemaphoreType.DMA(())
    params = pltpu.CompilerParams(vmem_limit_bytes=VMEM_BYTES)
    columns_scratch = pltpu.SMEM((prolong_columns.shape[1], LANES), jnp.int32)
    dense = pltpu.VMEM((3 * side // LANES, rows * BS, LANES), bf16)
    slots = prolong_columns.shape[1]
    packed = 16
    left, own, masks = pl.pallas_call(
        left_kernel,
        out_shape=(
            jax.ShapeDtypeStruct((3, 3 * side, rows * BS), bf16),
            jax.ShapeDtypeStruct((3 * side, 3 * side), f32),
            jax.ShapeDtypeStruct((2 * rows * slots, packed, 3 * side), bf16),
        ),
        in_specs=[smem, hbm, hbm, hbm],
        out_specs=(vmem, vmem, vmem),
        scratch_shapes=[
            pltpu.VMEM(matrix_blocks.shape, bf16),
            pltpu.VMEM(prolong_blocks.shape, bf16),
            columns_scratch, columns_scratch, columns_scratch,
            pltpu.VMEM((3 * rows * BS // LANES, rows * BS, LANES), bf16),
            dense,
            sem, sem, sem, sem, sem,
        ],
        compiler_params=params,
        name="left_kernel",
    )(matrix_turned, columns_turned, matrix_kept, prolong_kept)

    to_before, stay, to_after = pl.pallas_call(
        right_kernel,
        out_shape=(
            jax.ShapeDtypeStruct((side, 5 * side), bf16),
            jax.ShapeDtypeStruct((side, 5 * side), f32),
            jax.ShapeDtypeStruct((side, 5 * side), bf16),
        ),
        in_specs=[vmem, vmem, vmem, vmem, vmem],
        out_specs=(vmem, vmem, vmem),
        compiler_params=params,
        name="right_kernel",
    )(before_blocks, after_blocks, masks, left, own)

    from_before = shifted(to_after, BOTH, 1)
    from_after = shifted(to_before, BOTH, -1)

    def widen(part, offset):
        return jnp.pad(part.astype(f32), ((0, 0), (offset * side, (2 - offset) * side)))

    total = widen(from_before, 0) + widen(stay, 1) + widen(from_after, 2)
    owned = total.astype(bf16).reshape(aggregates, BS, 7 * side)
    shape = (lax.axis_size("grp") * aggregates, BS, 7 * side)
    below, above, far = [shifted(owned, "grp", by) for by in (1, -1, 2)]
    out = placed(None, [owned, above, far], (0, 1, 2), (0, 0, 0), shape)
    return placed(out, [below], (-1,), (0,), shape)


def solution(mesh):
    placed = (
        P(("grp", "row"), None, None),
        P(("grp", "row"), None),
        P(("grp", "row"), None, None),
        P(),
    )
    return jax.shard_map(
        per_device, mesh=mesh, in_specs=placed, out_specs=P("row", None, None), check_vma=False
    )
```

```python
import jax
import jax.numpy as jnp
from jax import lax
from jax.experimental import pallas as pl
from jax.experimental.pallas import tpu as pltpu
from jax.sharding import PartitionSpec as P

AGS = 8
BS = 64
LANES = 128
CHUNK = 4
VMEM_BYTES = 48 * 1024 * 1024
BOTH = ("grp", "row")


def shifted(value, axis, by):
    peers = lax.axis_size(axis)
    return lax.ppermute(value, axis, [(i, (i + by) % peers) for i in range(peers)])


def wrapped(value, total):
    value = jnp.where(value < 0, value + total, value)
    return jnp.where(value >= total, value - total, value)


def spread(blocks_ref, row, column_of, dense_ref):
    low = lax.broadcasted_iota(jnp.int32, (BS, LANES), 1) < BS
    for slot in range(blocks_ref.shape[2] // BS):
        block = blocks_ref[row, :, slot * BS : (slot + 1) * BS]
        twice = jnp.concatenate([block, block], axis=1)
        column = column_of(slot)
        place = dense_ref.at[column // 2, row * BS : (row + 1) * BS, :]
        place[...] = jnp.where(low == (column % 2 == 0), twice, place[...])


def joined(dense_ref, first, count):
    return jnp.concatenate([dense_ref[first + t] for t in range(count)], axis=1)


def columns_copy(columns_hbm, columns_ref, sem, group, rows):
    first = group * rows // LANES * LANES
    return pltpu.make_async_copy(
        columns_hbm.at[:, pl.ds(pl.multiple_of(first, LANES), LANES)], columns_ref, sem
    )


def mark(columns_ref, group, groups, rows, mask_ref, first):
    aggregates = rows // AGS
    slots = columns_ref.shape[0]
    block = lax.broadcasted_iota(jnp.int32, mask_ref.shape[1:], 1) // BS
    lane = lax.rem(group * rows, LANES)
    low = lax.rem(lax.broadcasted_iota(jnp.int32, mask_ref.shape[1:], 1), LANES) < BS
    for row in range(rows):
        for slot in range(0, slots, 2):
            even, odd = [
                wrapped(columns_ref[n, lane + row] - (group - 1) * aggregates, groups * aggregates)
                for n in (slot, slot + 1)
            ]
            for n, column in enumerate((jnp.where(low, even, odd), jnp.where(low, odd, even))):
                mask_ref[first + row * slots + slot + n] = jnp.where(
                    block == column, 1.0, 0.0
                ).astype(mask_ref.dtype)


def dense_rows(blocks_ref, mask_ref, first, start, count):
    width = blocks_ref.shape[2]
    slots = width // BS
    packed = mask_ref.shape[1]
    parts = []
    for row in range(start, start + count):
        twice = []
        for pair in range(slots // 2):
            both = blocks_ref[row, :, pair * LANES : (pair + 1) * LANES]
            swapped = jnp.concatenate([both[:, BS:], both[:, :BS]], axis=1)
            twice += [both, swapped]
        tiles = []
        for tile in range(mask_ref.shape[2] // LANES):
            total = None
            for slot in range(slots):
                mask = mask_ref[
                    first + row * slots + slot, :, tile * LANES : (tile + 1) * LANES
                ]
                term = twice[slot].reshape(BS // packed, packed, LANES) * mask[None]
                total = term if total is None else total + term
            tiles.append(total.reshape(BS, LANES))
        parts.append(jnp.concatenate(tiles, axis=1))
    return jnp.concatenate(parts, axis=0)


def left_kernel(
    a_cols_ref, columns_hbm, a_hbm, p_hbm, left_ref, own_ref, mask_ref,
    a_ref, p_ref, p_cols_ref, before_cols_ref, after_cols_ref, dense_a_ref, dense_p_ref,
    a_sem, p_sem, c_sem, before_sem, after_sem,
):
    rows = a_ref.shape[0]
    group = lax.axis_index(BOTH)
    groups = lax.axis_size(BOTH)
    fine_total = groups * rows
    aggregates = rows // AGS
    copy_c = columns_copy(columns_hbm, p_cols_ref, c_sem, group, rows)
    copy_p = pltpu.make_async_copy(p_hbm, p_ref, p_sem)
    copy_a = pltpu.make_async_copy(a_hbm, a_ref, a_sem)
    before = wrapped(group - 1, groups)
    after = wrapped(group + 1, groups)
    copy_before = columns_copy(columns_hbm, before_cols_ref, before_sem, before, rows)
    copy_after = columns_copy(columns_hbm, after_cols_ref, after_sem, after, rows)
    copy_c.start()
    copy_p.start()
    copy_a.start()
    copy_before.start()
    copy_after.start()
    dense_p_ref[...] = jnp.zeros_like(dense_p_ref)
    dense_a_ref[...] = jnp.zeros_like(dense_a_ref)
    copy_c.wait()
    copy_p.wait()
    lane = lax.rem(group * rows, LANES)
    for row in range(rows):
        spread(
            p_ref, row,
            lambda slot: wrapped(
                p_cols_ref[slot, lane + row] - (group - 1) * aggregates, groups * aggregates
            ),
            dense_p_ref,
        )
    tiles = dense_p_ref.shape[0]
    p_dense = joined(dense_p_ref, 0, tiles)
    p_turned = p_dense.T
    copy_a.wait()
    for row in range(rows):
        spread(
            a_ref, row,
            lambda slot: wrapped(a_cols_ref[slot, row] - (group - 1) * rows, fine_total),
            dense_a_ref,
        )
    parts = left_ref.shape[0]
    per_part = dense_a_ref.shape[0] // parts
    for part in range(parts):
        a_dense = joined(dense_a_ref, part * per_part, per_part)
        left_ref[part] = jnp.dot(
            p_turned, a_dense, preferred_element_type=jnp.float32
        ).astype(jnp.bfloat16)
    own_ref[...] = jnp.dot(left_ref[1], p_dense, preferred_element_type=jnp.float32)
    copy_before.wait()
    copy_after.wait()
    mark(before_cols_ref, before, groups, rows, mask_ref, 0)
    mark(after_cols_ref, after, groups, rows, mask_ref, mask_ref.shape[0] // 2)


def right_kernel(
    before_ref, after_ref, mask_ref, left_ref, own_ref, to_before_ref, stay_ref, to_after_ref
):
    def term(part, blocks_ref, first_mask):
        total = None
        for start in range(0, blocks_ref.shape[0], CHUNK):
            dense = dense_rows(blocks_ref, mask_ref, first_mask, start, CHUNK)
            inner = left_ref[part, :, start * BS : (start + CHUNK) * BS]
            product = jnp.dot(inner, dense, preferred_element_type=jnp.float32)
            total = product if total is None else total + product
        return total

    first = term(0, before_ref, 0)
    last = term(2, after_ref, mask_ref.shape[0] // 2)
    own = own_ref[...]
    step = LANES
    summed = jnp.concatenate(
        [
            first[:, :step],
            first[:, step : 2 * step] + own[:, :step],
            first[:, 2 * step :] + own[:, step : 2 * step] + last[:, :step],
            own[:, 2 * step :] + last[:, step : 2 * step],
            last[:, 2 * step :],
        ],
        axis=1,
    )
    side = stay_ref.shape[0]
    to_before_ref[...] = summed[:side].astype(to_before_ref.dtype)
    stay_ref[...] = summed[side : 2 * side]
    to_after_ref[...] = summed[2 * side :].astype(to_after_ref.dtype)


def placed(out, pieces, offsets, rows, shape):
    given = () if out is None else (out,)

    def place_kernel(*refs):
        out_hbm, sems = refs[-2], refs[-1]
        own = lax.axis_index("grp")
        size = lax.axis_size("grp")
        per_member = shape[0] // size
        copies = []
        for n in range(len(pieces)):
            first = lax.rem(own + offsets[n] + size, size) * per_member + rows[n]
            place = out_hbm.at[pl.ds(first, pieces[n].shape[0])]
            copies.append(pltpu.make_async_copy(refs[len(given) + n], place, sems.at[n]))
        for copy in copies:
            copy.start()
        for copy in copies:
            copy.wait()

    vmem = pl.BlockSpec(memory_space=pltpu.VMEM)
    hbm = pl.BlockSpec(memory_space=pltpu.HBM)
    return pl.pallas_call(
        place_kernel,
        out_shape=jax.ShapeDtypeStruct(shape, jnp.bfloat16),
        in_specs=[hbm] * len(given) + [vmem] * len(pieces),
        out_specs=hbm,
        scratch_shapes=[pltpu.SemaphoreType.DMA((len(pieces),))],
        input_output_aliases={0: 0} if given else {},
        compiler_params=pltpu.CompilerParams(vmem_limit_bytes=VMEM_BYTES),
        name="place_kernel",
    )(*given, *pieces)


def per_device(matrix_blocks, matrix_columns, prolong_blocks, prolong_columns):
    rows = matrix_blocks.shape[0]
    aggregates = rows // AGS
    side = aggregates * BS
    before_blocks = shifted(prolong_blocks, BOTH, 1)
    after_blocks = shifted(prolong_blocks, BOTH, -1)
    columns_turned = pltpu.with_memory_space_constraint(prolong_columns.T, pltpu.HBM)
    matrix_kept = pltpu.with_memory_space_constraint(matrix_blocks, pltpu.HBM)
    prolong_kept = pltpu.with_memory_space_constraint(prolong_blocks, pltpu.HBM)
    matrix_turned = pltpu.with_memory_space_constraint(matrix_columns.T, pltpu.HBM)

    bf16 = jnp.bfloat16
    f32 = jnp.float32
    smem = pl.BlockSpec(memory_space=pltpu.SMEM)
    vmem = pl.BlockSpec(memory_space=pltpu.VMEM)
    hbm = pl.BlockSpec(memory_space=pltpu.HBM)
    sem = pltpu.SemaphoreType.DMA(())
    params = pltpu.CompilerParams(vmem_limit_bytes=VMEM_BYTES)
    columns_scratch = pltpu.SMEM((prolong_columns.shape[1], LANES), jnp.int32)
    dense = pltpu.VMEM((3 * side // LANES, rows * BS, LANES), bf16)
    slots = prolong_columns.shape[1]
    packed = 16
    left, own, masks = pl.pallas_call(
        left_kernel,
        out_shape=(
            jax.ShapeDtypeStruct((3, 3 * side, rows * BS), bf16),
            jax.ShapeDtypeStruct((3 * side, 3 * side), f32),
            jax.ShapeDtypeStruct((2 * rows * slots, packed, 3 * side), bf16),
        ),
        in_specs=[smem, hbm, hbm, hbm],
        out_specs=(vmem, vmem, vmem),
        scratch_shapes=[
            pltpu.VMEM(matrix_blocks.shape, bf16),
            pltpu.VMEM(prolong_blocks.shape, bf16),
            columns_scratch, columns_scratch, columns_scratch,
            pltpu.VMEM((3 * rows * BS // LANES, rows * BS, LANES), bf16),
            dense,
            sem, sem, sem, sem, sem,
        ],
        compiler_params=params,
        name="left_kernel",
    )(matrix_turned, columns_turned, matrix_kept, prolong_kept)

    to_before, stay, to_after = pl.pallas_call(
        right_kernel,
        out_shape=(
            jax.ShapeDtypeStruct((side, 5 * side), bf16),
            jax.ShapeDtypeStruct((side, 5 * side), f32),
            jax.ShapeDtypeStruct((side, 5 * side), bf16),
        ),
        in_specs=[vmem, vmem, vmem, vmem, vmem],
        out_specs=(vmem, vmem, vmem),
        compiler_params=params,
        name="right_kernel",
    )(before_blocks, after_blocks, masks, left, own)

    from_before = shifted(to_after, BOTH, 1)
    from_after = shifted(to_before, BOTH, -1)

    def widen(part, offset):
        return jnp.pad(part.astype(f32), ((0, 0), (offset * side, (2 - offset) * side)))

    total = widen(from_before, 0) + widen(stay, 1) + widen(from_after, 2)
    owned = total.astype(bf16).reshape(aggregates, BS, 7 * side)
    shape = (lax.axis_size("grp") * aggregates, BS, 7 * side)
    below, above, far = [shifted(owned, "grp", by) for by in (1, -1, 2)]
    out = placed(None, [owned, above, far], (0, 1, 2), (0, 0, 0), shape)
    return placed(out, [below], (-1,), (0,), shape)


def solution(mesh):
    placed = (
        P(("grp", "row"), None, None),
        P(("grp", "row"), None),
        P(("grp", "row"), None, None),
        P(),
    )
    return jax.shard_map(
        per_device, mesh=mesh, in_specs=placed, out_specs=P("row", None, None), check_vma=False
    )
```
